256 devices in a mesh: dp: 16 (over z, core), expert: 16 (over x, y).
Axes of the slice: x: 4, y: 4, z: 8, core: 2. Of those that a mesh axis runs over, the one named last changes fastest.
Arguments:
- saved_input: bfloat16 [32768, 2048], P(('dp', 'expert')), parts along dimension 0, may hold values from -6 to 6
- grad_out: bfloat16 [32768, 2048], P(('dp', 'expert')), parts along dimension 0, may hold values from -6 to 6
- routes: int32 [32768, 8], P(('dp', 'expert')), parts along dimension 0, may hold values from 0 to 15, all different within a row
- route_gates: bfloat16 [32768, 8], P(('dp', 'expert')), parts along dimension 0, may hold values from 0.049804688 to 0.5
- gate_proj: bfloat16 [16, 2048, 768], P('expert'), may hold values from -0.125 to 0.125
- up_proj: bfloat16 [16, 2048, 768], P('expert'), may hold values from -0.125 to 0.125
- down_proj: bfloat16 [16, 768, 2048], P('expert'), may hold values from -0.21875 to 0.21875
Outputs:
- grad_in: bfloat16 [32768, 2048], P(('dp', 'expert')), parts along dimension 0
The draws below stay inside these ranges and needn't reach their ends.
There are 16 independent parts, one for each index of `dp`. The reference program is written for one: setup_inputs(seed, part) draws one part's arguments, and reference() takes and returns one part's arrays. A program takes and returns all parts, laid end to end along the dimension named above; an argument that names none is the same for every part. Nothing has to cross between parts.
Inputs may be any that keep to these rules, and one draw needn't show every extreme that they name: `routes`: each token names 8 different experts, and every expert is named by some token.
All inputs are finite; a program needn't handle non-finite values.
Results may differ from the reference program's by a relative error of at most 0.0057.
Values may be sent and summed in bfloat16 or wider, within the bound.
A program may use at most 128 MiB of HBM per device.

```python
import jax
import jax.numpy as jnp
from jax import lax

D = 2048
FF = 768
EXPERTS = 16
TOP = 8
TOK_DEV = 128
CAP = 56
TOKENS = 2048


def block_scale(key, shape, split, low, top_value):
    loudness = 1.0
    for axis_at, blocks in split:
        draws = jax.random.uniform(jax.random.fold_in(jax.random.fold_in(key, 6), axis_at), (blocks,), jnp.float32, low / len(split), top_value / len(split))
        loudness = loudness * jnp.repeat(jnp.exp(draws), shape[axis_at] // blocks).reshape((-1,) + (1,) * (len(shape) - 1 - axis_at))
    return loudness


def different_ones(key, rows, amount, top, lift):
    sequence = jax.random.permutation(jax.random.fold_in(key, 1), amount)
    favour = sequence
    for power in range(3):
        favour = favour * favour // amount
    favour = favour * lift // amount
    chance = jax.random.randint(jax.random.fold_in(key, 2), (rows, amount), 0, 4096) + favour
    fixed_rows = jax.random.permutation(jax.random.fold_in(key, 3), rows)[jnp.arange(amount) % rows]
    chance = jnp.where(jnp.arange(rows)[:, None] == fixed_rows[None, :], 1 << 14, chance)
    score = chance * amount + jnp.arange(amount)
    return lax.top_k(score.astype(jnp.int32), top)[1].astype(jnp.int32)


def centred(own_key, extent, spread, most, pieces=(), kind=jnp.bfloat16):
    result = jax.random.normal(own_key, extent, jnp.float32) * spread
    if len(pieces) > 0:
        result = block_scale(own_key, extent, pieces, -0.22, 0.18) * result
    return jnp.clip(result, min=-most, max=most).astype(kind)


def setup_inputs(seed: int = 0, part: int = 0) -> dict:
    splits = jax.random.split(jax.random.key(seed), 8)
    own_keys = jax.random.split(jax.random.fold_in(splits[7], part), 8)
    return {
        "saved_input": centred(own_keys[0], (TOKENS, D), 1.0, 6.0, ((0, 16),)),
        "grad_out": centred(own_keys[1], (TOKENS, D), 1.0, 6.0, ((0, 16),)),
        "routes": different_ones(own_keys[2], TOKENS, EXPERTS, TOP, 4096),
        "route_gates": jnp.clip(0.049804688 + 0.4501953 * jax.random.uniform(own_keys[3], (TOKENS, TOP), jnp.float32) ** block_scale(own_keys[3], (TOKENS, TOP), ((0, 16),), -0.2, 0.2), 0.049804688, 0.5).astype(jnp.bfloat16),
        "gate_proj": centred(splits[4], (EXPERTS, D, FF), D ** -0.5, 0.125, ((0, 16),)),
        "up_proj": centred(splits[5], (EXPERTS, D, FF), D ** -0.5, 0.125, ((0, 16),)),
        "down_proj": centred(splits[6], (EXPERTS, FF, D), FF ** -0.5, 0.21875, ((0, 16),)),
    }


def pair_ranks(routing):
    groups = routing.shape[0]
    ordered = jnp.swapaxes(routing, 1, 2).reshape(groups, -1)
    labels = jnp.arange(EXPERTS, dtype=jnp.int32)
    matches = (ordered[..., None] == labels).astype(jnp.int32)
    earlier = jnp.cumsum(matches, axis=1) - matches
    ranking = jnp.sum(earlier * matches, axis=-1)
    return ordered, ranking


def expert_rows(packed):
    input_rows, grad_rows, gate_rows, gate_weight, up_weight, down_weight = packed
    gate_pre = jnp.dot(input_rows, gate_weight, preferred_element_type=jnp.float32)
    up_pre = jnp.dot(input_rows, up_weight, preferred_element_type=jnp.float32)
    back_grad = jnp.dot(grad_rows, down_weight.T, preferred_element_type=jnp.float32)
    scaled = gate_rows.astype(jnp.float32)[:, None] * back_grad
    sigmoid_gate = jax.nn.sigmoid(gate_pre)
    gate_grad = (scaled * up_pre * sigmoid_gate * (1.0 + gate_pre * (1.0 - sigmoid_gate))).astype(jnp.bfloat16)
    up_grad = (scaled * gate_pre * sigmoid_gate).astype(jnp.bfloat16)
    summed = jnp.dot(gate_grad, gate_weight.T, preferred_element_type=jnp.float32)
    summed = summed + jnp.dot(up_grad, up_weight.T, preferred_element_type=jnp.float32)
    return summed.astype(jnp.bfloat16)


def reference(saved_input, grad_out, routes, route_gates, gate_proj, up_proj, down_proj):
    groups = TOKENS // TOK_DEV
    routing = routes.reshape(groups, TOK_DEV, TOP)
    ordered, ranking = pair_ranks(routing)
    pair_index = jnp.arange(TOP * TOK_DEV, dtype=jnp.int32)
    token_local = pair_index % TOK_DEV
    choice_index = pair_index // TOK_DEV
    group_index = jnp.arange(groups, dtype=jnp.int32)[:, None]
    token_global = group_index * TOK_DEV + token_local[None, :]
    slot_total = groups * CAP
    slot_of = jnp.where(ranking < CAP, ordered * slot_total + group_index * CAP + ranking, EXPERTS * slot_total)
    flat_slot = slot_of.reshape(-1).astype(jnp.int32)
    source_row = jnp.full((EXPERTS * slot_total,), TOKENS, jnp.int32)
    source_row = source_row.at[flat_slot].set(token_global.reshape(-1).astype(jnp.int32), mode="drop")
    gate_pairs = route_gates[token_global, choice_index[None, :]]
    gate_buffer = jnp.zeros((EXPERTS * slot_total,), jnp.bfloat16)
    gate_buffer = gate_buffer.at[flat_slot].set(gate_pairs.reshape(-1), mode="drop")
    zero_row = jnp.zeros((1, D), jnp.bfloat16)
    input_rows = jnp.concatenate([saved_input, zero_row], 0)[source_row].reshape(EXPERTS, slot_total, D)
    grad_rows = jnp.concatenate([grad_out, zero_row], 0)[source_row].reshape(EXPERTS, slot_total, D)
    gate_rows = gate_buffer.reshape(EXPERTS, slot_total)
    expert_out = lax.map(expert_rows, (input_rows, grad_rows, gate_rows, gate_proj, up_proj, down_proj))
    flat_rows = jnp.concatenate([expert_out.reshape(-1, D), zero_row], 0)
    picked = flat_rows[flat_slot].reshape(groups, TOP, TOK_DEV, D)
    summed = jnp.sum(picked.astype(jnp.float32), axis=1)
    return summed.reshape(TOKENS, D).astype(jnp.bfloat16)
```

```python
import jax
import jax.numpy as jnp
from jax import lax
from jax.sharding import PartitionSpec as P

CAP = 56
CHUNKS = 2


def pair_ranks(ordered, experts):
    labels = jnp.arange(experts, dtype=jnp.int32)
    matches = (ordered[..., None] == labels).astype(jnp.int32)
    earlier = jnp.cumsum(matches, axis=-2) - matches
    return jnp.sum(earlier * matches, axis=-1)


def expert_rows(input_rows, grad_rows, gate_rows, gate_proj, up_proj, down_proj):
    gate_pre = jnp.einsum("nd,df->nf", input_rows, gate_proj, preferred_element_type=jnp.float32)
    up_pre = jnp.einsum("nd,df->nf", input_rows, up_proj, preferred_element_type=jnp.float32)
    back_grad = jnp.einsum("nd,fd->nf", grad_rows, down_proj, preferred_element_type=jnp.float32)
    scaled = gate_rows.astype(jnp.float32)[:, None] * back_grad
    sigmoid_gate = jax.nn.sigmoid(gate_pre)
    gate_grad = (scaled * up_pre * sigmoid_gate * (1.0 + gate_pre * (1.0 - sigmoid_gate))).astype(
        jnp.bfloat16
    )
    up_grad = (scaled * gate_pre * sigmoid_gate).astype(jnp.bfloat16)
    summed = jnp.einsum("nf,df->nd", gate_grad, gate_proj, preferred_element_type=jnp.float32)
    summed = summed + jnp.einsum("nf,df->nd", up_grad, up_proj, preferred_element_type=jnp.float32)
    return summed.astype(jnp.bfloat16)


def body(saved_input, grad_out, routes, route_gates, gate_proj, up_proj, down_proj):
    devices = lax.axis_size("expert")
    local_experts = gate_proj.shape[0]
    experts = devices * local_experts
    tok_rows, features = saved_input.shape
    top_count = routes.shape[1]
    part = CAP // CHUNKS
    chunk_slots = devices * part * local_experts
    ordered = jnp.swapaxes(routes, 0, 1).reshape(-1)
    ranking = pair_ranks(ordered, experts).reshape(top_count, tok_rows)
    ordered = ordered.reshape(top_count, tok_rows)
    owner_dev = ordered // local_experts
    local_slot = ordered % local_experts
    chunk_of = ranking // part
    within = ranking % part
    slot_in_chunk = (owner_dev * part + within) * local_experts + local_slot
    pair_gates = jnp.swapaxes(route_gates, 0, 1).astype(jnp.float32)
    rows_both = jnp.stack([saved_input, grad_out])
    slot_ids = jnp.arange(chunk_slots, dtype=jnp.int32)
    total = jnp.zeros((tok_rows, features), jnp.float32)
    for c in range(CHUNKS):
        slot_c = jnp.where(chunk_of == c, slot_in_chunk, -1)
        pick = slot_c[:, None, :] == slot_ids[None, :, None]
        pick_f = pick.astype(jnp.float32)
        select = jnp.any(pick, axis=0).astype(jnp.bfloat16)
        send_rows = jnp.einsum(
            "st,ntd->nsd", select, rows_both, preferred_element_type=jnp.float32
        ).astype(jnp.bfloat16)
        send_gate = jnp.einsum("kst,kt->s", pick_f, pair_gates).astype(jnp.bfloat16)
        send_rows = send_rows.reshape(2, devices, part * local_experts, features)
        send_gate = send_gate.reshape(devices, part * local_experts)
        got_rows = lax.all_to_all(send_rows, "expert", split_axis=1, concat_axis=1, tiled=True)
        got_gate = lax.all_to_all(send_gate, "expert", split_axis=0, concat_axis=0, tiled=True)
        got_x = got_rows[0].reshape(devices * part, local_experts, features)
        got_g = got_rows[1].reshape(devices * part, local_experts, features)
        got_w = got_gate.reshape(devices * part, local_experts)
        outs = []
        for e in range(local_experts):
            outs.append(
                expert_rows(
                    got_x[:, e], got_g[:, e], got_w[:, e], gate_proj[e], up_proj[e], down_proj[e]
                )
            )
        out_rows = jnp.stack(outs, axis=1).reshape(devices, part * local_experts, features)
        back = lax.all_to_all(out_rows, "expert", split_axis=0, concat_axis=0, tiled=True)
        back = back.reshape(chunk_slots, features)
        total = total + jnp.einsum(
            "st,sd->td", select, back, preferred_element_type=jnp.float32
        )
    return total.astype(jnp.bfloat16)


def solution(mesh):
    in_specs = (
        P(("dp", "expert"), None),
        P(("dp", "expert"), None),
        P(("dp", "expert"), None),
        P(("dp", "expert"), None),
        P("expert", None, None),
        P("expert", None, None),
        P("expert", None, None),
    )
    out_specs = P(("dp", "expert"), None)
    return jax.shard_map(body, mesh=mesh, in_specs=in_specs, out_specs=out_specs, check_vma=False)
```

```python
import functools

import jax
import jax.numpy as jnp
from jax import lax
from jax.experimental import pallas as pl
from jax.experimental.pallas import tpu as pltpu
from jax.sharding import PartitionSpec as P

CAP = 56
LANES = 128
MESH_ID = pl.DeviceIdType.MESH


def pair_ranks(ordered, experts):
    labels = jnp.arange(experts, dtype=jnp.int32)
    matches = (ordered[..., None] == labels).astype(jnp.int32)
    earlier = jnp.cumsum(matches, axis=-2) - matches
    return jnp.sum(earlier * matches, axis=-1)


def expert_block(x, g, w, wg_ref, wu_ref, wd_ref):
    nt = (((1,), (1,)), ((), ()))
    gate_pre = jnp.dot(x, wg_ref[...], preferred_element_type=jnp.float32)
    up_pre = jnp.dot(x, wu_ref[...], preferred_element_type=jnp.float32)
    back_grad = lax.dot_general(g, wd_ref[...], nt, preferred_element_type=jnp.float32)
    scaled = w[:, 0:1].astype(jnp.float32) * back_grad
    sigmoid_gate = 1.0 / (1.0 + jnp.exp(-gate_pre))
    gate_grad = (scaled * up_pre * sigmoid_gate * (1.0 + gate_pre * (1.0 - sigmoid_gate))).astype(
        jnp.bfloat16
    )
    up_grad = (scaled * gate_pre * sigmoid_gate).astype(jnp.bfloat16)
    summed = lax.dot_general(gate_grad, wg_ref[...], nt, preferred_element_type=jnp.float32)
    summed = summed + lax.dot_general(up_grad, wu_ref[...], nt, preferred_element_type=jnp.float32)
    return summed.astype(jnp.bfloat16)


def moe_kernel(n, sx, sg, sw, wg, wu, wd, ret, rx, rg, rw, ob, dsend, drecv, bsend, brecv, lsem):
    me = lax.axis_index("expert")

    def peer(d):
        return {"expert": lax.rem(me + d, n)}

    def back_peer(d):
        return {"expert": lax.rem(me + n - d, n)}

    barrier = pltpu.get_barrier_semaphore()
    for d in range(1, n):
        pl.semaphore_signal(barrier, 1, device_id=peer(d), device_id_type=MESH_ID)
    pl.semaphore_wait(barrier, n - 1)

    srcs = (sx, sg, sw)
    dsts = (rx, rg, rw)

    def dispatch(k, d):
        return pltpu.make_async_remote_copy(
            srcs[k].at[d], dsts[k].at[d], dsend.at[k, d], drecv.at[k, d],
            device_id=peer(d), device_id_type=MESH_ID,
        )

    def give_back(d):
        return pltpu.make_async_remote_copy(
            ob.at[d], ret.at[d], bsend.at[d], brecv.at[d],
            device_id=back_peer(d), device_id_type=MESH_ID,
        )

    local_in = [pltpu.make_async_copy(srcs[k].at[0], dsts[k].at[0], lsem.at[k]) for k in range(3)]
    for c in local_in:
        c.start()
    for d in range(1, n):
        for k in range(3):
            dispatch(k, d).start()

    for c in local_in:
        c.wait()
    ob[0] = expert_block(rx[0], rg[0], rw[0], wg, wu, wd)
    local_out = pltpu.make_async_copy(ob.at[0], ret.at[0], lsem.at[3])
    local_out.start()

    def step(d, carry):
        for k in range(3):
            dispatch(k, d).wait_recv()
        ob[d] = expert_block(rx[d], rg[d], rw[d], wg, wu, wd)
        give_back(d).start()
        return carry

    lax.fori_loop(1, n, step, 0)

    def drain(d, carry):
        for k in range(3):
            dispatch(k, d).wait_send()
        give_back(d).wait_send()
        give_back(d).wait_recv()
        return carry

    lax.fori_loop(1, n, drain, 0)
    local_out.wait()


def exchange(send_x, send_g, send_w, wg, wu, wd):
    n, cap, features = send_x.shape
    ff = wg.shape[1]
    vmem = pltpu.MemorySpace.VMEM
    flops = 2 * n * cap * features * ff * 5
    return pl.pallas_call(
        functools.partial(moe_kernel, n),
        out_shape=jax.ShapeDtypeStruct((n, cap, features), jnp.bfloat16),
        in_specs=[pl.BlockSpec(memory_space=pl.ANY)] * 3 + [pl.BlockSpec(memory_space=vmem)] * 3,
        out_specs=pl.BlockSpec(memory_space=pl.ANY),
        scratch_shapes=[
            pltpu.VMEM((n, cap, features), jnp.bfloat16),
            pltpu.VMEM((n, cap, features), jnp.bfloat16),
            pltpu.VMEM((n, cap, LANES), jnp.bfloat16),
            pltpu.VMEM((n, cap, features), jnp.bfloat16),
            pltpu.SemaphoreType.DMA((3, n)),
            pltpu.SemaphoreType.DMA((3, n)),
            pltpu.SemaphoreType.DMA((n,)),
            pltpu.SemaphoreType.DMA((n,)),
            pltpu.SemaphoreType.DMA((4,)),
        ],
        compiler_params=pltpu.CompilerParams(
            collective_id=0, has_side_effects=True, vmem_limit_bytes=60 * 1024 * 1024
        ),
        cost_estimate=pl.CostEstimate(
            flops=flops, transcendentals=n * cap * ff, bytes_accessed=n * cap * features * 2 * 4
        ),
    )(send_x, send_g, send_w, wg, wu, wd)


def body(saved_input, grad_out, routes, route_gates, gate_proj, up_proj, down_proj):
    devices = lax.axis_size("expert")
    local_experts = gate_proj.shape[0]
    assert local_experts == 1
    experts = devices * local_experts
    tok_rows, features = saved_input.shape
    top_count = routes.shape[1]
    slot_count = devices * CAP
    me = lax.axis_index("expert")
    ordered = jnp.swapaxes(routes, 0, 1).reshape(-1)
    ranking = pair_ranks(ordered, experts).reshape(top_count, tok_rows)
    ordered = ordered.reshape(top_count, tok_rows)
    distance = lax.rem(ordered - me + devices, devices)
    slot_of = jnp.where(ranking < CAP, distance * CAP + ranking, -1)
    slot_ids = jnp.arange(slot_count, dtype=jnp.int32)
    pick = slot_of[:, None, :] == slot_ids[None, :, None]
    select = jnp.any(pick, axis=0).astype(jnp.bfloat16)
    pair_gates = jnp.swapaxes(route_gates, 0, 1).astype(jnp.float32)
    send_gate = jnp.einsum("kst,kt->s", pick.astype(jnp.float32), pair_gates)
    send_w = jnp.broadcast_to(send_gate[:, None], (slot_count, LANES)).astype(jnp.bfloat16)
    send_x = jnp.dot(select, saved_input, preferred_element_type=jnp.float32).astype(jnp.bfloat16)
    send_g = jnp.dot(select, grad_out, preferred_element_type=jnp.float32).astype(jnp.bfloat16)
    shape3 = (devices, CAP, features)
    back = exchange(
        send_x.reshape(shape3),
        send_g.reshape(shape3),
        send_w.reshape(devices, CAP, LANES),
        gate_proj[0],
        up_proj[0],
        down_proj[0],
    )
    total = jnp.einsum(
        "st,sd->td", select, back.reshape(slot_count, features), preferred_element_type=jnp.float32
    )
    return total.astype(jnp.bfloat16)


def solution(mesh):
    in_specs = (
        P(("dp", "expert"), None),
        P(("dp", "expert"), None),
        P(("dp", "expert"), None),
        P(("dp", "expert"), None),
        P("expert", None, None),
        P("expert", None, None),
        P("expert", None, None),
    )
    out_specs = P(("dp", "expert"), None)
    return jax.shard_map(body, mesh=mesh, in_specs=in_specs, out_specs=out_specs, check_vma=False)
```

```python
import functools

import jax
import jax.numpy as jnp
from jax import lax
from jax.experimental import pallas as pl
from jax.experimental.pallas import tpu as pltpu
from jax.sharding import PartitionSpec as P

CAP = 56
LANES = 128
PIECES = 8
MESH_ID = pl.DeviceIdType.MESH


def pair_ranks(ordered, experts):
    labels = jnp.arange(experts, dtype=jnp.int32)
    matches = (ordered[..., None] == labels).astype(jnp.int32)
    earlier = jnp.cumsum(matches, axis=-2) - matches
    return jnp.sum(earlier * matches, axis=-1)


def expert_block(x, g, w, wg_ref, wu_ref, wd_ref):
    nt = (((1,), (1,)), ((), ()))
    gate_pre = jnp.dot(x, wg_ref[...], preferred_element_type=jnp.float32)
    up_pre = jnp.dot(x, wu_ref[...], preferred_element_type=jnp.float32)
    back_grad = lax.dot_general(g, wd_ref[...], nt, preferred_element_type=jnp.float32)
    scaled = w[:, 0:1].astype(jnp.float32) * back_grad
    sigmoid_gate = 1.0 / (1.0 + jnp.exp(-gate_pre))
    gate_grad = (scaled * up_pre * sigmoid_gate * (1.0 + gate_pre * (1.0 - sigmoid_gate))).astype(
        jnp.bfloat16
    )
    up_grad = (scaled * gate_pre * sigmoid_gate).astype(jnp.bfloat16)
    summed = lax.dot_general(gate_grad, wg_ref[...], nt, preferred_element_type=jnp.float32)
    summed = summed + lax.dot_general(up_grad, wu_ref[...], nt, preferred_element_type=jnp.float32)
    return summed.astype(jnp.bfloat16)


def moe_kernel(n, sx, sg, sw, wg, wu, wd, ret, rx, rg, rw, ob, dsend, drecv, bsend, brecv, lsem):
    me = lax.axis_index("expert")

    def peer(d):
        return {"expert": lax.rem(me + d, n)}

    def back_peer(d):
        return {"expert": lax.rem(me + n - d, n)}

    barrier = pltpu.get_barrier_semaphore()
    for d in range(1, n):
        pl.semaphore_signal(barrier, 1, device_id=peer(d), device_id_type=MESH_ID)
    pl.semaphore_wait(barrier, n - 1)

    srcs = (sx, sg, sw)
    dsts = (rx, rg, rw)

    def dispatch(k, d, cols=None):
        src, dst = srcs[k].at[d], dsts[k].at[d]
        if cols is not None:
            src, dst = src.at[:, cols], dst.at[:, cols]
        return pltpu.make_async_remote_copy(
            src, dst, dsend.at[k, d], drecv.at[k, d],
            device_id=peer(d), device_id_type=MESH_ID,
        )

    def give_back(d, cols=None):
        src, dst = ob.at[d], ret.at[d]
        if cols is not None:
            src, dst = src.at[:, cols], dst.at[:, cols]
        return pltpu.make_async_remote_copy(
            src, dst, bsend.at[d], brecv.at[d],
            device_id=back_peer(d), device_id_type=MESH_ID,
        )

    features = sx.shape[-1]
    width = features // PIECES
    pieces = [pl.ds(j * width, width) for j in range(PIECES)]

    local_in = [pltpu.make_async_copy(srcs[k].at[0], dsts[k].at[0], lsem.at[k]) for k in range(3)]
    for c in local_in:
        c.start()
    for d in range(1, n):
        for cols in pieces:
            dispatch(0, d, cols).start()
            dispatch(1, d, cols).start()
        dispatch(2, d).start()

    for c in local_in:
        c.wait()
    ob[0] = expert_block(rx[0], rg[0], rw[0], wg, wu, wd)
    local_out = pltpu.make_async_copy(ob.at[0], ret.at[0], lsem.at[3])
    local_out.start()

    def step(d, carry):
        for k in range(3):
            dispatch(k, d).wait_recv()
        ob[d] = expert_block(rx[d], rg[d], rw[d], wg, wu, wd)
        for cols in pieces:
            give_back(d, cols).start()
        return carry

    lax.fori_loop(1, n, step, 0)

    def drain(d, carry):
        for k in range(3):
            dispatch(k, d).wait_send()
        give_back(d).wait_send()
        give_back(d).wait_recv()
        return carry

    lax.fori_loop(1, n, drain, 0)
    local_out.wait()


def exchange(send_x, send_g, send_w, wg, wu, wd):
    n, cap, features = send_x.shape
    ff = wg.shape[1]
    vmem = pltpu.MemorySpace.VMEM
    flops = 2 * n * cap * features * ff * 5
    return pl.pallas_call(
        functools.partial(moe_kernel, n),
        out_shape=jax.ShapeDtypeStruct((n, cap, features), jnp.bfloat16),
        in_specs=[pl.BlockSpec(memory_space=pl.ANY)] * 3 + [pl.BlockSpec(memory_space=vmem)] * 3,
        out_specs=pl.BlockSpec(memory_space=pl.ANY),
        scratch_shapes=[
            pltpu.VMEM((n, cap, features), jnp.bfloat16),
            pltpu.VMEM((n, cap, features), jnp.bfloat16),
            pltpu.VMEM((n, cap, LANES), jnp.bfloat16),
            pltpu.VMEM((n, cap, features), jnp.bfloat16),
            pltpu.SemaphoreType.DMA((3, n)),
            pltpu.SemaphoreType.DMA((3, n)),
            pltpu.SemaphoreType.DMA((n,)),
            pltpu.SemaphoreType.DMA((n,)),
            pltpu.SemaphoreType.DMA((4,)),
        ],
        compiler_params=pltpu.CompilerParams(
            collective_id=0, has_side_effects=True, vmem_limit_bytes=60 * 1024 * 1024
        ),
        cost_estimate=pl.CostEstimate(
            flops=flops, transcendentals=n * cap * ff, bytes_accessed=n * cap * features * 2 * 4
        ),
    )(send_x, send_g, send_w, wg, wu, wd)


def body(saved_input, grad_out, routes, route_gates, gate_proj, up_proj, down_proj):
    devices = lax.axis_size("expert")
    local_experts = gate_proj.shape[0]
    assert local_experts == 1
    experts = devices * local_experts
    tok_rows, features = saved_input.shape
    top_count = routes.shape[1]
    slot_count = devices * CAP
    me = lax.axis_index("expert")
    ordered = jnp.swapaxes(routes, 0, 1).reshape(-1)
    ranking = pair_ranks(ordered, experts).reshape(top_count, tok_rows)
    ordered = ordered.reshape(top_count, tok_rows)
    distance = lax.rem(ordered - me + devices, devices)
    slot_of = jnp.where(ranking < CAP, distance * CAP + ranking, -1)
    slot_ids = jnp.arange(slot_count, dtype=jnp.int32)
    pick = slot_of[:, None, :] == slot_ids[None, :, None]
    select = jnp.any(pick, axis=0).astype(jnp.bfloat16)
    pair_gates = jnp.swapaxes(route_gates, 0, 1).astype(jnp.float32)
    send_gate = jnp.einsum("kst,kt->s", pick.astype(jnp.float32), pair_gates)
    send_w = jnp.broadcast_to(send_gate[:, None], (slot_count, LANES)).astype(jnp.bfloat16)
    send_x = jnp.dot(select, saved_input, preferred_element_type=jnp.float32).astype(jnp.bfloat16)
    send_g = jnp.dot(select, grad_out, preferred_element_type=jnp.float32).astype(jnp.bfloat16)
    shape3 = (devices, CAP, features)
    back = exchange(
        send_x.reshape(shape3),
        send_g.reshape(shape3),
        send_w.reshape(devices, CAP, LANES),
        gate_proj[0],
        up_proj[0],
        down_proj[0],
    )
    total = jnp.einsum(
        "st,sd->td", select, back.reshape(slot_count, features), preferred_element_type=jnp.float32
    )
    return total.astype(jnp.bfloat16)


def solution(mesh):
    in_specs = (
        P(("dp", "expert"), None),
        P(("dp", "expert"), None),
        P(("dp", "expert"), None),
        P(("dp", "expert"), None),
        P("expert", None, None),
        P("expert", None, None),
        P("expert", None, None),
    )
    out_specs = P(("dp", "expert"), None)
    return jax.shard_map(body, mesh=mesh, in_specs=in_specs, out_specs=out_specs, check_vma=False)
```

```python
import functools

import jax
import jax.numpy as jnp
from jax import lax
from jax.experimental import pallas as pl
from jax.experimental.pallas import tpu as pltpu
from jax.sharding import PartitionSpec as P

CAP = 56
LANES = 128
PIECES = 7
MESH_ID = pl.DeviceIdType.MESH


def pair_ranks(ordered, experts):
    labels = jnp.arange(experts, dtype=jnp.int32)
    matches = (ordered[..., None] == labels).astype(jnp.int32)
    earlier = jnp.cumsum(matches, axis=-2) - matches
    return jnp.sum(earlier * matches, axis=-1)


def expert_block(x, g, w, wg_ref, wu_ref, wd_ref):
    nt = (((1,), (1,)), ((), ()))
    gate_pre = jnp.dot(x, wg_ref[...], preferred_element_type=jnp.float32)
    up_pre = jnp.dot(x, wu_ref[...], preferred_element_type=jnp.float32)
    back_grad = lax.dot_general(g, wd_ref[...], nt, preferred_element_type=jnp.float32)
    scaled = w[:, 0:1].astype(jnp.float32) * back_grad
    sigmoid_gate = 1.0 / (1.0 + jnp.exp(-gate_pre))
    gate_grad = (scaled * up_pre * sigmoid_gate * (1.0 + gate_pre * (1.0 - sigmoid_gate))).astype(
        jnp.bfloat16
    )
    up_grad = (scaled * gate_pre * sigmoid_gate).astype(jnp.bfloat16)
    summed = lax.dot_general(gate_grad, wg_ref[...], nt, preferred_element_type=jnp.float32)
    summed = summed + lax.dot_general(up_grad, wu_ref[...], nt, preferred_element_type=jnp.float32)
    return summed.astype(jnp.bfloat16)


def moe_kernel(n, sx, sg, sw, wg, wu, wd, ret, rx, rg, rw, ob, dsend, drecv, bsend, brecv, lsem):
    me = lax.axis_index("expert")

    def peer(d):
        return {"expert": lax.rem(me + d, n)}

    def back_peer(d):
        return {"expert": lax.rem(me + n - d, n)}

    barrier = pltpu.get_barrier_semaphore()
    for d in range(1, n):
        pl.semaphore_signal(barrier, 1, device_id=peer(d), device_id_type=MESH_ID)
    pl.semaphore_wait(barrier, n - 1)

    srcs = (sx, sg, sw)
    dsts = (rx, rg, rw)

    def dispatch(k, d, cols=None):
        src, dst = srcs[k].at[d], dsts[k].at[d]
        if cols is not None:
            src, dst = src.at[cols], dst.at[cols]
        return pltpu.make_async_remote_copy(
            src, dst, dsend.at[k, d], drecv.at[k, d],
            device_id=peer(d), device_id_type=MESH_ID,
        )

    def give_back(d, cols=None):
        src, dst = ob.at[d], ret.at[d]
        if cols is not None:
            src, dst = src.at[cols], dst.at[cols]
        return pltpu.make_async_remote_copy(
            src, dst, bsend.at[d], brecv.at[d],
            device_id=back_peer(d), device_id_type=MESH_ID,
        )

    height = sx.shape[1] // PIECES
    pieces = [pl.ds(j * height, height) for j in range(PIECES)]

    local_in = [pltpu.make_async_copy(srcs[k].at[0], dsts[k].at[0], lsem.at[k]) for k in range(3)]
    for c in local_in:
        c.start()
    for d in range(1, n):
        for cols in pieces:
            dispatch(0, d, cols).start()
            dispatch(1, d, cols).start()
        dispatch(2, d).start()

    for c in local_in:
        c.wait()
    ob[0] = expert_block(rx[0], rg[0], rw[0], wg, wu, wd)
    local_out = pltpu.make_async_copy(ob.at[0], ret.at[0], lsem.at[3])
    local_out.start()

    def step(d, carry):
        for k in range(3):
            dispatch(k, d).wait_recv()
        ob[d] = expert_block(rx[d], rg[d], rw[d], wg, wu, wd)
        for cols in pieces:
            give_back(d, cols).start()
        return carry

    lax.fori_loop(1, n, step, 0)

    def drain(d, carry):
        for k in range(3):
            dispatch(k, d).wait_send()
        give_back(d).wait_send()
        give_back(d).wait_recv()
        return carry

    lax.fori_loop(1, n, drain, 0)
    local_out.wait()


def exchange(send_x, send_g, send_w, wg, wu, wd):
    n, cap, features = send_x.shape
    ff = wg.shape[1]
    vmem = pltpu.MemorySpace.VMEM
    flops = 2 * n * cap * features * ff * 5
    return pl.pallas_call(
        functools.partial(moe_kernel, n),
        out_shape=jax.ShapeDtypeStruct((n, cap, features), jnp.bfloat16),
        in_specs=[pl.BlockSpec(memory_space=pl.ANY)] * 3 + [pl.BlockSpec(memory_space=vmem)] * 3,
        out_specs=pl.BlockSpec(memory_space=pl.ANY),
        scratch_shapes=[
            pltpu.VMEM((n, cap, features), jnp.bfloat16),
            pltpu.VMEM((n, cap, features), jnp.bfloat16),
            pltpu.VMEM((n, cap, LANES), jnp.bfloat16),
            pltpu.VMEM((n, cap, features), jnp.bfloat16),
            pltpu.SemaphoreType.DMA((3, n)),
            pltpu.SemaphoreType.DMA((3, n)),
            pltpu.SemaphoreType.DMA((n,)),
            pltpu.SemaphoreType.DMA((n,)),
            pltpu.SemaphoreType.DMA((4,)),
        ],
        compiler_params=pltpu.CompilerParams(
            collective_id=0, has_side_effects=True, vmem_limit_bytes=60 * 1024 * 1024
        ),
        cost_estimate=pl.CostEstimate(
            flops=flops, transcendentals=n * cap * ff, bytes_accessed=n * cap * features * 2 * 4
        ),
    )(send_x, send_g, send_w, wg, wu, wd)


def body(saved_input, grad_out, routes, route_gates, gate_proj, up_proj, down_proj):
    devices = lax.axis_size("expert")
    local_experts = gate_proj.shape[0]
    assert local_experts == 1
    experts = devices * local_experts
    tok_rows, features = saved_input.shape
    top_count = routes.shape[1]
    slot_count = devices * CAP
    me = lax.axis_index("expert")
    ordered = jnp.swapaxes(routes, 0, 1).reshape(-1)
    ranking = pair_ranks(ordered, experts).reshape(top_count, tok_rows)
    ordered = ordered.reshape(top_count, tok_rows)
    distance = lax.rem(ordered - me + devices, devices)
    slot_of = jnp.where(ranking < CAP, distance * CAP + ranking, -1)
    slot_ids = jnp.arange(slot_count, dtype=jnp.int32)
    pick = slot_of[:, None, :] == slot_ids[None, :, None]
    select = jnp.any(pick, axis=0).astype(jnp.bfloat16)
    pair_gates = jnp.swapaxes(route_gates, 0, 1).astype(jnp.float32)
    send_gate = jnp.einsum("kst,kt->s", pick.astype(jnp.float32), pair_gates)
    send_w = jnp.broadcast_to(send_gate[:, None], (slot_count, LANES)).astype(jnp.bfloat16)
    send_x = jnp.dot(select, saved_input, preferred_element_type=jnp.float32).astype(jnp.bfloat16)
    send_g = jnp.dot(select, grad_out, preferred_element_type=jnp.float32).astype(jnp.bfloat16)
    shape3 = (devices, CAP, features)
    back = exchange(
        send_x.reshape(shape3),
        send_g.reshape(shape3),
        send_w.reshape(devices, CAP, LANES),
        gate_proj[0],
        up_proj[0],
        down_proj[0],
    )
    total = jnp.einsum(
        "st,sd->td", select, back.reshape(slot_count, features), preferred_element_type=jnp.float32
    )
    return total.astype(jnp.bfloat16)


def solution(mesh):
    in_specs = (
        P(("dp", "expert"), None),
        P(("dp", "expert"), None),
        P(("dp", "expert"), None),
        P(("dp", "expert"), None),
        P("expert", None, None),
        P("expert", None, None),
        P("expert", None, None),
    )
    out_specs = P(("dp", "expert"), None)
    return jax.shard_map(body, mesh=mesh, in_specs=in_specs, out_specs=out_specs, check_vma=False)
```

```python
import functools

import jax
import jax.numpy as jnp
from jax import lax
from jax.experimental import pallas as pl
from jax.experimental.pallas import tpu as pltpu
from jax.sharding import PartitionSpec as P

CAP = 56
LANES = 128
PIECES = 7
MESH_ID = pl.DeviceIdType.MESH


def pair_ranks(ordered, experts):
    labels = jnp.arange(experts, dtype=jnp.int32)
    matches = (ordered[..., None] == labels).astype(jnp.int32)
    earlier = jnp.cumsum(matches, axis=-2) - matches
    return jnp.sum(earlier * matches, axis=-1)


def expert_block(x, g, w, wg_ref, wu_ref, wd_ref):
    nt = (((1,), (1,)), ((), ()))
    gate_pre = jnp.dot(x, wg_ref[...], preferred_element_type=jnp.float32)
    up_pre = jnp.dot(x, wu_ref[...], preferred_element_type=jnp.float32)
    back_grad = lax.dot_general(g, wd_ref[...], nt, preferred_element_type=jnp.float32)
    scaled = w[:, 0:1].astype(jnp.float32) * back_grad
    sigmoid_gate = 1.0 / (1.0 + jnp.exp(-gate_pre))
    gate_grad = (scaled * up_pre * sigmoid_gate * (1.0 + gate_pre * (1.0 - sigmoid_gate))).astype(
        jnp.bfloat16
    )
    up_grad = (scaled * gate_pre * sigmoid_gate).astype(jnp.bfloat16)
    summed = lax.dot_general(gate_grad, wg_ref[...], nt, preferred_element_type=jnp.float32)
    summed = summed + lax.dot_general(up_grad, wu_ref[...], nt, preferred_element_type=jnp.float32)
    return summed.astype(jnp.bfloat16)


def moe_kernel(n, sx, sg, sw, wg, wu, wd, ret, rx, rg, rw, ob, dsend, drecv, bsend, brecv, lsem):
    me = lax.axis_index("expert")

    def peer(d):
        return {"expert": lax.rem(me + d, n)}

    def back_peer(d):
        return {"expert": lax.rem(me + n - d, n)}

    barrier = pltpu.get_barrier_semaphore()
    for d in range(1, n):
        pl.semaphore_signal(barrier, 1, device_id=peer(d), device_id_type=MESH_ID)
    pl.semaphore_wait(barrier, n - 1)

    srcs = (sx, sg, sw)
    dsts = (rx, rg, rw)

    def dispatch(k, d, cols=None):
        src, dst = srcs[k].at[d], dsts[k].at[d]
        if cols is not None:
            src, dst = src.at[cols], dst.at[cols]
        return pltpu.make_async_remote_copy(
            src, dst, dsend.at[k, d], drecv.at[k, d],
            device_id=peer(d), device_id_type=MESH_ID,
        )

    def give_back(d, cols=None):
        src, dst = ob.at[d], ret.at[d]
        if cols is not None:
            src, dst = src.at[cols], dst.at[cols]
        return pltpu.make_async_remote_copy(
            src, dst, bsend.at[d], brecv.at[d],
            device_id=back_peer(d), device_id_type=MESH_ID,
        )

    height = sx.shape[1] // PIECES
    pieces = [pl.ds(j * height, height) for j in range(PIECES)]

    local_in = [pltpu.make_async_copy(srcs[k].at[0], dsts[k].at[0], lsem.at[k]) for k in range(3)]
    for c in local_in:
        c.start()
    for d in range(1, n):
        dispatch(2, d).start()
    for cols in pieces:
        for k in range(2):
            for d in range(1, n):
                dispatch(k, d, cols).start()

    for c in local_in:
        c.wait()
    ob[0] = expert_block(rx[0], rg[0], rw[0], wg, wu, wd)
    local_out = pltpu.make_async_copy(ob.at[0], ret.at[0], lsem.at[3])
    local_out.start()

    def step(d, carry):
        for k in range(3):
            dispatch(k, d).wait_recv()
        ob[d] = expert_block(rx[d], rg[d], rw[d], wg, wu, wd)
        for cols in pieces:
            give_back(d, cols).start()
        return carry

    lax.fori_loop(1, n, step, 0)

    def drain(d, carry):
        for k in range(3):
            dispatch(k, d).wait_send()
        give_back(d).wait_send()
        give_back(d).wait_recv()
        return carry

    lax.fori_loop(1, n, drain, 0)
    local_out.wait()


def exchange(send_x, send_g, send_w, wg, wu, wd):
    n, cap, features = send_x.shape
    ff = wg.shape[1]
    vmem = pltpu.MemorySpace.VMEM
    flops = 2 * n * cap * features * ff * 5
    return pl.pallas_call(
        functools.partial(moe_kernel, n),
        out_shape=jax.ShapeDtypeStruct((n, cap, features), jnp.bfloat16),
        in_specs=[pl.BlockSpec(memory_space=pl.ANY)] * 3 + [pl.BlockSpec(memory_space=vmem)] * 3,
        out_specs=pl.BlockSpec(memory_space=pl.ANY),
        scratch_shapes=[
            pltpu.VMEM((n, cap, features), jnp.bfloat16),
            pltpu.VMEM((n, cap, features), jnp.bfloat16),
            pltpu.VMEM((n, cap, LANES), jnp.bfloat16),
            pltpu.VMEM((n, cap, features), jnp.bfloat16),
            pltpu.SemaphoreType.DMA((3, n)),
            pltpu.SemaphoreType.DMA((3, n)),
            pltpu.SemaphoreType.DMA((n,)),
            pltpu.SemaphoreType.DMA((n,)),
            pltpu.SemaphoreType.DMA((4,)),
        ],
        compiler_params=pltpu.CompilerParams(
            collective_id=0, has_side_effects=True, vmem_limit_bytes=60 * 1024 * 1024
        ),
        cost_estimate=pl.CostEstimate(
            flops=flops, transcendentals=n * cap * ff, bytes_accessed=n * cap * features * 2 * 4
        ),
    )(send_x, send_g, send_w, wg, wu, wd)


def body(saved_input, grad_out, routes, route_gates, gate_proj, up_proj, down_proj):
    devices = lax.axis_size("expert")
    local_experts = gate_proj.shape[0]
    assert local_experts == 1
    experts = devices * local_experts
    tok_rows, features = saved_input.shape
    top_count = routes.shape[1]
    slot_count = devices * CAP
    me = lax.axis_index("expert")
    ordered = jnp.swapaxes(routes, 0, 1).reshape(-1)
    ranking = pair_ranks(ordered, experts).reshape(top_count, tok_rows)
    ordered = ordered.reshape(top_count, tok_rows)
    distance = lax.rem(ordered - me + devices, devices)
    slot_of = jnp.where(ranking < CAP, distance * CAP + ranking, -1)
    slot_ids = jnp.arange(slot_count, dtype=jnp.int32)
    pick = slot_of[:, None, :] == slot_ids[None, :, None]
    select = jnp.any(pick, axis=0).astype(jnp.bfloat16)
    pair_gates = jnp.swapaxes(route_gates, 0, 1).astype(jnp.float32)
    send_gate = jnp.einsum("kst,kt->s", pick.astype(jnp.float32), pair_gates)
    send_w = jnp.broadcast_to(send_gate[:, None], (slot_count, LANES)).astype(jnp.bfloat16)
    send_x = jnp.dot(select, saved_input, preferred_element_type=jnp.float32).astype(jnp.bfloat16)
    send_g = jnp.dot(select, grad_out, preferred_element_type=jnp.float32).astype(jnp.bfloat16)
    shape3 = (devices, CAP, features)
    back = exchange(
        send_x.reshape(shape3),
        send_g.reshape(shape3),
        send_w.reshape(devices, CAP, LANES),
        gate_proj[0],
        up_proj[0],
        down_proj[0],
    )
    total = jnp.einsum(
        "st,sd->td", select, back.reshape(slot_count, features), preferred_element_type=jnp.float32
    )
    return total.astype(jnp.bfloat16)


def solution(mesh):
    in_specs = (
        P(("dp", "expert"), None),
        P(("dp", "expert"), None),
        P(("dp", "expert"), None),
        P(("dp", "expert"), None),
        P("expert", None, None),
        P("expert", None, None),
        P("expert", None, None),
    )
    out_specs = P(("dp", "expert"), None)
    return jax.shard_map(body, mesh=mesh, in_specs=in_specs, out_specs=out_specs, check_vma=False)
```

```python
import functools

import jax
import jax.numpy as jnp
from jax import lax
from jax.experimental import pallas as pl
from jax.experimental.pallas import tpu as pltpu
from jax.sharding import PartitionSpec as P

CAP = 56
LANES = 128
TILE = 8
PIECES = 7
MESH_ID = pl.DeviceIdType.MESH


def pair_ranks(routing, experts):
    choices, tokens = routing.shape
    labels = jnp.arange(experts, dtype=jnp.int32)
    onehot = (routing[:, :, None] == labels).astype(jnp.int32)
    per_choice = jnp.sum(onehot, axis=1)
    before = jnp.cumsum(per_choice, axis=0) - per_choice
    from_before = jnp.sum(onehot * before[:, None, :], axis=2)
    same = routing[:, :, None] == routing[:, None, :]
    earlier = lax.broadcasted_iota(jnp.int32, (tokens, tokens), 1) < lax.broadcasted_iota(
        jnp.int32, (tokens, tokens), 0
    )
    within = jnp.sum((same & earlier[None]).astype(jnp.int32), axis=2)
    return from_before + within


def expert_block(x, g, gate_col, wg_ref, wu_ref, wd_ref):
    nt = (((1,), (1,)), ((), ()))
    gate_pre = jnp.dot(x, wg_ref[...], preferred_element_type=jnp.float32)
    up_pre = jnp.dot(x, wu_ref[...], preferred_element_type=jnp.float32)
    back_grad = lax.dot_general(g, wd_ref[...], nt, preferred_element_type=jnp.float32)
    scaled = gate_col * back_grad
    sigmoid_gate = 1.0 / (1.0 + jnp.exp(-gate_pre))
    gate_grad = (scaled * up_pre * sigmoid_gate * (1.0 + gate_pre * (1.0 - sigmoid_gate))).astype(
        jnp.bfloat16
    )
    up_grad = (scaled * gate_pre * sigmoid_gate).astype(jnp.bfloat16)
    summed = lax.dot_general(gate_grad, wg_ref[...], nt, preferred_element_type=jnp.float32)
    summed = summed + lax.dot_general(up_grad, wu_ref[...], nt, preferred_element_type=jnp.float32)
    return summed.astype(jnp.bfloat16)


def moe_kernel(n, xin, gin, slot_rows, slot_cols, sw, wg, wu, wd, out, sx, sg, rx, rg, rw, ob, rb,
               sel, selt, dsend, drecv, bsend, brecv, lsem):
    me = lax.axis_index("expert")
    cap = sx.shape[0] // n
    block = 2 * cap

    def peer(d):
        return {"expert": lax.rem(me + d, n)}

    def back_peer(d):
        return {"expert": lax.rem(me + n - d, n)}

    barrier = pltpu.get_barrier_semaphore()
    for d in range(1, n):
        pl.semaphore_signal(barrier, 1, device_id=peer(d), device_id_type=MESH_ID)

    choices = slot_rows.shape[0]
    slot_iota = lax.broadcasted_iota(jnp.int32, sel.shape, 0)
    hit = slot_rows[0:1, :] == slot_iota
    for k in range(1, choices):
        hit = hit | (slot_rows[k:k + 1, :] == slot_iota)
    sel[...] = hit.astype(sel.dtype)

    def build_selt():
        lane_iota = lax.broadcasted_iota(jnp.int32, selt.shape, 1)
        hit_t = slot_cols[:, 0:1] == lane_iota
        for k in range(1, choices):
            hit_t = hit_t | (slot_cols[:, k:k + 1] == lane_iota)
        selt[...] = hit_t.astype(selt.dtype)

    def build(dst, src):
        for b in range(n // 2):
            span = pl.ds(b * block, block)
            dst[span, :] = jnp.dot(
                sel[span, :], src[...], preferred_element_type=jnp.float32
            ).astype(dst.dtype)

    srcs = (sx, sg, sw)
    dsts = (rx, rg, rw)
    height = cap // PIECES

    def rows(d, j=None):
        if j is None:
            return pl.ds(d * cap, cap)
        return pl.ds(d * cap + j * height, height)

    def gate_rows(d):
        return pl.ds(d * TILE, TILE)

    def dispatch(k, d, j=None):
        span = gate_rows(d) if k == 2 else rows(d, j)
        return pltpu.make_async_remote_copy(
            srcs[k].at[span], dsts[k].at[span], dsend.at[k, d], drecv.at[k, d],
            device_id=peer(d), device_id_type=MESH_ID,
        )

    def give_back(d, j=None):
        return pltpu.make_async_remote_copy(
            ob.at[rows(d, j)], rb.at[rows(d, j)], bsend.at[d], brecv.at[d],
            device_id=back_peer(d), device_id_type=MESH_ID,
        )

    def start_rows(k):
        for j in range(PIECES):
            for d in range(1, n):
                dispatch(k, d, j).start()

    build(sx, xin)
    pl.semaphore_wait(barrier, n - 1)
    local_in = [
        pltpu.make_async_copy(srcs[k].at[rows(0) if k < 2 else gate_rows(0)],
                              dsts[k].at[rows(0) if k < 2 else gate_rows(0)], lsem.at[k])
        for k in range(3)
    ]
    local_in[0].start()
    local_in[2].start()
    for d in range(1, n):
        dispatch(2, d).start()
    start_rows(0)
    build(sg, gin)
    local_in[1].start()
    start_rows(1)
    build_selt()

    def compute(q):
        span = pl.ds(pl.multiple_of(q * block, block), block)
        tiles = rw[pl.ds(pl.multiple_of(q * 2 * TILE, 2 * TILE), 2 * TILE), :]
        cols = jnp.transpose(tiles)
        gate_col = jnp.concatenate([cols[:cap, 0:1], cols[:cap, TILE:TILE + 1]], axis=0)
        ob[span, :] = expert_block(rx[span, :], rg[span, :], gate_col, wg, wu, wd)

    for c in local_in:
        c.wait()
    for k in range(3):
        dispatch(k, 1).wait_recv()
    compute(0)
    local_out = pltpu.make_async_copy(ob.at[rows(0)], rb.at[rows(0)], lsem.at[3])
    local_out.start()
    for j in range(PIECES):
        give_back(1, j).start()

    def step(q, carry):
        for d in (2 * q, 2 * q + 1):
            for k in range(3):
                dispatch(k, d).wait_recv()
        compute(q)
        for j in range(PIECES):
            for d in (2 * q, 2 * q + 1):
                give_back(d, j).start()
        return carry

    lax.fori_loop(1, n // 2, step, 0)

    def drain(d, carry):
        for k in range(3):
            dispatch(k, d).wait_send()
        give_back(d).wait_send()
        give_back(d).wait_recv()
        return carry

    lax.fori_loop(1, n, drain, 0)
    local_out.wait()
    out[...] = jnp.dot(selt[...], rb[...], preferred_element_type=jnp.float32).astype(out.dtype)


def exchange(saved_input, grad_out, slot_of, send_w, wg, wu, wd, n, slots):
    tok_rows, features = saved_input.shape
    ff = wg.shape[1]
    vmem = pltpu.MemorySpace.VMEM
    flops = 2 * slots * features * ff * 5 + 2 * 3 * slots * tok_rows * features
    big = pltpu.VMEM((slots, features), jnp.bfloat16)
    return pl.pallas_call(
        functools.partial(moe_kernel, n),
        out_shape=jax.ShapeDtypeStruct((tok_rows, features), jnp.bfloat16),
        in_specs=[pl.BlockSpec(memory_space=vmem)] * 8,
        out_specs=pl.BlockSpec(memory_space=vmem),
        scratch_shapes=[
            big,
            big,
            big,
            big,
            pltpu.VMEM((n * TILE, LANES), jnp.float32),
            big,
            big,
            pltpu.VMEM((slots, tok_rows), jnp.bfloat16),
            pltpu.VMEM((tok_rows, slots), jnp.bfloat16),
            pltpu.SemaphoreType.DMA((3, n)),
            pltpu.SemaphoreType.DMA((3, n)),
            pltpu.SemaphoreType.DMA((n,)),
            pltpu.SemaphoreType.DMA((n,)),
            pltpu.SemaphoreType.DMA((4,)),
        ],
        compiler_params=pltpu.CompilerParams(
            collective_id=0, has_side_effects=True, vmem_limit_bytes=62 * 1024 * 1024
        ),
        cost_estimate=pl.CostEstimate(
            flops=flops, transcendentals=slots * ff, bytes_accessed=slots * features * 2 * 3
        ),
    )(saved_input, grad_out, slot_of, slot_of.T, send_w, wg, wu, wd)


def body(saved_input, grad_out, routes, route_gates, gate_proj, up_proj, down_proj):
    devices = lax.axis_size("expert")
    local_experts = gate_proj.shape[0]
    assert local_experts == 1
    experts = devices * local_experts
    tok_rows, features = saved_input.shape
    top_count = routes.shape[1]
    slot_count = devices * CAP
    me = lax.axis_index("expert")
    ordered = jnp.swapaxes(routes, 0, 1).reshape(-1)
    ordered = ordered.reshape(top_count, tok_rows)
    ranking = pair_ranks(ordered, experts)
    distance = lax.rem(ordered - me + devices, devices)
    slot_of = jnp.where(ranking < CAP, distance * CAP + ranking, -1)
    slot_ids = jnp.arange(slot_count, dtype=jnp.int32)
    pick = slot_of[:, None, :] == slot_ids[None, :, None]
    pair_gates = jnp.swapaxes(route_gates, 0, 1).astype(jnp.float32)
    send_gate = jnp.einsum("kst,kt->s", pick.astype(jnp.float32), pair_gates)
    send_w = jnp.zeros((devices, TILE, LANES), jnp.float32)
    send_w = send_w.at[:, 0, :CAP].set(send_gate.reshape(devices, CAP)).reshape(devices * TILE, LANES)
    assert devices % 2 == 0
    return exchange(
        saved_input, grad_out, slot_of, send_w, gate_proj[0], up_proj[0], down_proj[0], devices, slot_count
    )


def solution(mesh):
    in_specs = (
        P(("dp", "expert"), None),
        P(("dp", "expert"), None),
        P(("dp", "expert"), None),
        P(("dp", "expert"), None),
        P("expert", None, None),
        P("expert", None, None),
        P("expert", None, None),
    )
    out_specs = P(("dp", "expert"), None)
    return jax.shard_map(body, mesh=mesh, in_specs=in_specs, out_specs=out_specs, check_vma=False)
```

```python
import functools

import jax
import jax.numpy as jnp
from jax import lax
from jax.experimental import pallas as pl
from jax.experimental.pallas import tpu as pltpu
from jax.sharding import PartitionSpec as P

CAP = 56
LANES = 128
TILE = 8
PIECES = 7
MESH_ID = pl.DeviceIdType.MESH


def pair_ranks(ordered):
    count = ordered.shape[0]
    same = ordered[:, None] == ordered[None, :]
    earlier = lax.broadcasted_iota(jnp.int32, (count, count), 1) < lax.broadcasted_iota(
        jnp.int32, (count, count), 0
    )
    return jnp.sum((same & earlier).astype(jnp.int32), axis=1)


def expert_block(x, g, gate_col, wg_ref, wu_ref, wd_ref):
    nt = (((1,), (1,)), ((), ()))
    gate_pre = jnp.dot(x, wg_ref[...], preferred_element_type=jnp.float32)
    up_pre = jnp.dot(x, wu_ref[...], preferred_element_type=jnp.float32)
    back_grad = lax.dot_general(g, wd_ref[...], nt, preferred_element_type=jnp.float32)
    scaled = gate_col * back_grad
    sigmoid_gate = 1.0 / (1.0 + jnp.exp(-gate_pre))
    gate_grad = (scaled * up_pre * sigmoid_gate * (1.0 + gate_pre * (1.0 - sigmoid_gate))).astype(
        jnp.bfloat16
    )
    up_grad = (scaled * gate_pre * sigmoid_gate).astype(jnp.bfloat16)
    summed = lax.dot_general(gate_grad, wg_ref[...], nt, preferred_element_type=jnp.float32)
    summed = summed + lax.dot_general(up_grad, wu_ref[...], nt, preferred_element_type=jnp.float32)
    return summed.astype(jnp.bfloat16)


def moe_kernel(n, xin, gin, slot_rows, slot_cols, sw, wg, wu, wd, out, sx, sg, rx, rg, rw, ob, rb,
               sel, selt, dsend, drecv, bsend, brecv, lsem):
    me = lax.axis_index("expert")
    cap = sx.shape[0] // n
    block = 2 * cap

    def peer(d):
        return {"expert": lax.rem(me + d, n)}

    def back_peer(d):
        return {"expert": lax.rem(me + n - d, n)}

    barrier = pltpu.get_barrier_semaphore()
    for d in range(1, n):
        pl.semaphore_signal(barrier, 1, device_id=peer(d), device_id_type=MESH_ID)

    choices = slot_rows.shape[0]
    slot_iota = lax.broadcasted_iota(jnp.int32, sel.shape, 0)
    hit = slot_rows[0:1, :] == slot_iota
    for k in range(1, choices):
        hit = hit | (slot_rows[k:k + 1, :] == slot_iota)
    sel[...] = hit.astype(sel.dtype)

    def build_selt():
        lane_iota = lax.broadcasted_iota(jnp.int32, selt.shape, 1)
        hit_t = slot_cols[:, 0:1] == lane_iota
        for k in range(1, choices):
            hit_t = hit_t | (slot_cols[:, k:k + 1] == lane_iota)
        selt[...] = hit_t.astype(selt.dtype)

    def build(dst, src):
        for b in range(n // 2):
            span = pl.ds(b * block, block)
            dst[span, :] = jnp.dot(
                sel[span, :], src[...], preferred_element_type=jnp.float32
            ).astype(dst.dtype)

    srcs = (sx, sg, sw)
    dsts = (rx, rg, rw)
    height = cap // PIECES

    def rows(d, j=None):
        if j is None:
            return pl.ds(d * cap, cap)
        return pl.ds(d * cap + j * height, height)

    def gate_rows(d):
        return pl.ds(d * TILE, TILE)

    def dispatch(k, d, j=None):
        span = gate_rows(d) if k == 2 else rows(d, j)
        return pltpu.make_async_remote_copy(
            srcs[k].at[span], dsts[k].at[span], dsend.at[k, d], drecv.at[k, d],
            device_id=peer(d), device_id_type=MESH_ID,
        )

    def give_back(d, j=None):
        return pltpu.make_async_remote_copy(
            ob.at[rows(d, j)], rb.at[rows(d, j)], bsend.at[d], brecv.at[d],
            device_id=back_peer(d), device_id_type=MESH_ID,
        )

    def start_rows(k):
        for j in range(PIECES):
            for d in range(1, n):
                dispatch(k, d, j).start()

    build(sx, xin)
    pl.semaphore_wait(barrier, n - 1)
    local_in = [
        pltpu.make_async_copy(srcs[k].at[rows(0) if k < 2 else gate_rows(0)],
                              dsts[k].at[rows(0) if k < 2 else gate_rows(0)], lsem.at[k])
        for k in range(3)
    ]
    local_in[0].start()
    local_in[2].start()
    for d in range(1, n):
        dispatch(2, d).start()
    start_rows(0)
    build(sg, gin)
    local_in[1].start()
    start_rows(1)
    build_selt()

    def compute(q):
        span = pl.ds(pl.multiple_of(q * block, block), block)
        tiles = rw[pl.ds(pl.multiple_of(q * 2 * TILE, 2 * TILE), 2 * TILE), :]
        cols = jnp.transpose(tiles)
        gate_col = jnp.concatenate([cols[:cap, 0:1], cols[:cap, TILE:TILE + 1]], axis=0)
        ob[span, :] = expert_block(rx[span, :], rg[span, :], gate_col, wg, wu, wd)

    for c in local_in:
        c.wait()
    for k in range(3):
        dispatch(k, 1).wait_recv()
    compute(0)
    local_out = pltpu.make_async_copy(ob.at[rows(0)], rb.at[rows(0)], lsem.at[3])
    local_out.start()
    for j in range(PIECES):
        give_back(1, j).start()

    def step(q, carry):
        for d in (2 * q, 2 * q + 1):
            for k in range(3):
                dispatch(k, d).wait_recv()
        compute(q)
        for j in range(PIECES):
            for d in (2 * q, 2 * q + 1):
                give_back(d, j).start()
        return carry

    lax.fori_loop(1, n // 2, step, 0)

    def drain(d, carry):
        for k in range(3):
            dispatch(k, d).wait_send()
        give_back(d).wait_send()
        give_back(d).wait_recv()
        return carry

    lax.fori_loop(1, n, drain, 0)
    local_out.wait()
    out[...] = jnp.dot(selt[...], rb[...], preferred_element_type=jnp.float32)


def exchange(saved_input, grad_out, slot_of, send_w, wg, wu, wd, n, slots):
    tok_rows, features = saved_input.shape
    ff = wg.shape[1]
    vmem = pltpu.MemorySpace.VMEM
    flops = 2 * slots * features * ff * 5 + 2 * 3 * slots * tok_rows * features
    big = pltpu.VMEM((slots, features), jnp.bfloat16)
    return pl.pallas_call(
        functools.partial(moe_kernel, n),
        out_shape=jax.ShapeDtypeStruct((tok_rows, features), jnp.float32),
        in_specs=[pl.BlockSpec(memory_space=vmem)] * 8,
        out_specs=pl.BlockSpec(memory_space=vmem),
        scratch_shapes=[
            big,
            big,
            big,
            big,
            pltpu.VMEM((n * TILE, LANES), jnp.float32),
            big,
            big,
            pltpu.VMEM((slots, tok_rows), jnp.bfloat16),
            pltpu.VMEM((tok_rows, slots), jnp.bfloat16),
            pltpu.SemaphoreType.DMA((3, n)),
            pltpu.SemaphoreType.DMA((3, n)),
            pltpu.SemaphoreType.DMA((n,)),
            pltpu.SemaphoreType.DMA((n,)),
            pltpu.SemaphoreType.DMA((4,)),
        ],
        compiler_params=pltpu.CompilerParams(
            collective_id=0, has_side_effects=True, vmem_limit_bytes=62 * 1024 * 1024
        ),
        cost_estimate=pl.CostEstimate(
            flops=flops, transcendentals=slots * ff, bytes_accessed=slots * features * 2 * 3
        ),
    )(saved_input, grad_out, slot_of, slot_of.T, send_w, wg, wu, wd)


def body(saved_input, grad_out, routes, route_gates, gate_proj, up_proj, down_proj):
    devices = lax.axis_size("expert")
    local_experts = gate_proj.shape[0]
    assert local_experts == 1
    experts = devices * local_experts
    tok_rows, features = saved_input.shape
    top_count = routes.shape[1]
    slot_count = devices * CAP
    me = lax.axis_index("expert")
    ordered = jnp.swapaxes(routes, 0, 1).reshape(-1)
    ranking = pair_ranks(ordered).reshape(top_count, tok_rows)
    ordered = ordered.reshape(top_count, tok_rows)
    distance = lax.rem(ordered - me + devices, devices)
    slot_of = jnp.where(ranking < CAP, distance * CAP + ranking, -1)
    slot_ids = jnp.arange(slot_count, dtype=jnp.int32)
    pick = slot_of[:, None, :] == slot_ids[None, :, None]
    pair_gates = jnp.swapaxes(route_gates, 0, 1).astype(jnp.float32)
    send_gate = jnp.einsum("kst,kt->s", pick.astype(jnp.float32), pair_gates)
    send_w = jnp.zeros((devices, TILE, LANES), jnp.float32)
    send_w = send_w.at[:, 0, :CAP].set(send_gate.reshape(devices, CAP)).reshape(devices * TILE, LANES)
    assert devices % 2 == 0
    total = exchange(
        saved_input, grad_out, slot_of, send_w, gate_proj[0], up_proj[0], down_proj[0], devices, slot_count
    )
    return total.astype(jnp.bfloat16)


def solution(mesh):
    in_specs = (
        P(("dp", "expert"), None),
        P(("dp", "expert"), None),
        P(("dp", "expert"), None),
        P(("dp", "expert"), None),
        P("expert", None, None),
        P("expert", None, None),
        P("expert", None, None),
    )
    out_specs = P(("dp", "expert"), None)
    return jax.shard_map(body, mesh=mesh, in_specs=in_specs, out_specs=out_specs, check_vma=False)
```
